512 devices in a mesh: grp: 32 (over z_hi, y, core), aux: 16 (over x, z_lo).
Axes of the slice: x: 4, y: 4, z: 16 (z_hi: 4, z_lo: 4; z = z_hi * 4 + z_lo), core: 2. Of those that a mesh axis runs over, the one named last changes fastest.
Arguments:
- half_ints: float32 [2560, 128, 1280], P('aux', 'grp'), may hold values from -0.9 to 0.9
- virt_coeff: float32 [1280, 640], P('aux'), may hold values from -0.15625 to 0.15625
- occ_energy: float32 [128], replicated, may hold values from -2 to -0.3
- vir_energy: float32 [640], replicated, may hold values from 0.1 to 3
- aux_sizes: int32 [16], replicated, may hold values from 1 to 160, 1920 in all
- pair_root: int32 [4], replicated, may hold values from 0 to 31
Outputs:
- gamma: float32 [2560, 81920], P(None, ('grp', 'aux'))
The draws below stay inside these ranges and needn't reach their ends.
Inputs may be any that keep to these rules, and one draw needn't show every extreme that they name: aux_sizes sums to 1920 and its largest entry is exactly 160.
All inputs are finite; a program needn't handle non-finite values.
Results may differ from the reference program's by a relative error of at most 0.0003.
Values sent between devices are 32-bit elements; how exact they have to be, the bound alone decides.
No kernel may reach another device: no remote copies, remote signals or barrier semaphores. Data moves between devices by JAX's collectives and lax.ppermute only.
A program may use at most 128 MiB of HBM per device.

```python
import math
import jax
import jax.numpy as jnp
import numpy as np
from jax import lax

NAO = 1280
NVIR = 640
NAUX = 1920
OCC_GRP = 4
NOCC = 128
PMAX = 160
NAUXPAD = 2560
N_GRP = 32
N_AUX = 16


def set_ends(entries, key, low, largest):
    spot = [jax.random.randint(jax.random.fold_in(key, axis), (), 0, length) for axis, length in enumerate(entries.shape)]
    main_axis = entries.shape.index(max(entries.shape))
    beside = spot[:main_axis] + [(spot[main_axis] + 1) % entries.shape[main_axis]] + spot[main_axis + 1:]
    return entries.at[tuple(spot)].set(low).at[tuple(beside)].set(largest)


def levels(key, dims, split, smallest, largest):
    def one(axis_at, blocks):
        draws = jax.random.uniform(jax.random.fold_in(jax.random.fold_in(key, 6), axis_at), (blocks,), jnp.float32, smallest / len(split), largest / len(split))
        return jnp.repeat(jnp.exp(draws), dims[axis_at] // blocks).reshape((-1,) + (1,) * (len(dims) - axis_at - 1))

    level = one(*split[0])
    for cut in split[1:]:
        level = level * one(*cut)
    return level


def profile(count, total, limit, slope):
    weights = [(1 << 20) // math.isqrt(standing ** slope) + 1 for standing in range(2, count + 1)]
    rest, holding = total - limit - (count - 1), [1] * (count - 1)
    while rest > 0:
        candidates = [i for i in range(count - 1) if holding[i] < limit]
        mass, left = sum([weights[i] for i in candidates]), rest
        for i in candidates:
            extra = min(limit - holding[i], max(1, left * weights[i] // mass), rest)
            holding[i] = holding[i] + extra
            rest = rest - extra
    return np.array([limit] + holding)


def ragged_sizes(key, count, total, reach, slope):
    if count == 2:
        one = jax.random.randint(key, (), max(1, total - reach), min(reach, total - 1) + 1)
        return jnp.stack([one, total - one])
    lengths = jnp.asarray(profile(count, total, reach, slope), jnp.int32)
    couples = (count - 1) // 2
    source_of, taker = lengths[1:1 + 2 * couples:2], lengths[2:2 + 2 * couples:2]
    margin = jnp.minimum(source_of - 1, reach - taker)
    shifted = jax.random.randint(jax.random.fold_in(key, 1), (couples,), 0, 1 << 20) % (margin + 1)
    lengths = lengths.at[1:1 + 2 * couples:2].set(source_of - shifted).at[2:2 + 2 * couples:2].set(taker + shifted)
    return lengths[jax.random.permutation(jax.random.fold_in(key, 2), count)]


def scatter_about(rng, shape, width, bound, cuts=(), kind=jnp.bfloat16):
    factor_of = levels(rng, shape, cuts, -0.22, 0.18) if cuts else 1.0
    result = jax.random.normal(rng, shape, jnp.float32) * width * factor_of
    return jnp.minimum(jnp.maximum(result, -bound), bound).astype(kind)


def setup_inputs(seed: int = 0) -> dict:
    key_of = jax.random.split(jax.random.key(seed), 7)
    return {
        "half_ints": scatter_about(key_of[0], (NAUXPAD, NOCC, NAO), 0.15, 0.9, ((0, 16), (1, 32)), jnp.float32),
        "virt_coeff": scatter_about(key_of[1], (NAO, NVIR), NAO ** -0.5, 0.15625, ((0, 16),), jnp.float32),
        "occ_energy": jnp.clip(jax.random.uniform(key_of[2], (NOCC,), jnp.float32, -2.0, -0.3), -2.0, -0.3),
        "vir_energy": jnp.clip(jax.random.uniform(key_of[3], (NVIR,), jnp.float32, 0.1, 3.0), 0.1, 3.0),
        "aux_sizes": ragged_sizes(key_of[4], N_AUX, NAUX, PMAX, 2).astype(jnp.int32),
        "pair_root": set_ends(jax.random.randint(key_of[5], (OCC_GRP,), 0, N_GRP), jax.random.fold_in(key_of[5], 1), 0, N_GRP - 1).astype(jnp.int32),
    }


def reference(half_ints, virt_coeff, occ_energy, vir_energy, aux_sizes, pair_root):
    aux_rows = jnp.arange(NAUXPAD, dtype=jnp.int32)
    live_rows = ((aux_rows % PMAX) < aux_sizes[aux_rows // PMAX]).astype(jnp.float32)
    transformed = jnp.einsum("pim,ma->pia", half_ints, virt_coeff, precision=lax.Precision.HIGHEST)
    transformed = transformed * live_rows[:, None, None]

    def per_orbital(orbital):
        slot = (orbital % OCC_GRP).astype(jnp.int32)
        partner = (pair_root[slot] * OCC_GRP + slot).astype(jnp.int32)
        own_vecs = lax.dynamic_index_in_dim(transformed, orbital, 1, keepdims=False)
        partner_vecs = lax.dynamic_index_in_dim(transformed, partner, 1, keepdims=False)
        pair_ints = lax.dot_general(own_vecs, partner_vecs, (((0,), (0,)), ((), ())), precision=lax.Precision.HIGHEST)
        denominator = occ_energy[orbital] + occ_energy[partner] - vir_energy[:, None] - vir_energy[None, :]
        amplitude = (2.0 * pair_ints - pair_ints.T) / denominator
        return jnp.dot(partner_vecs, amplitude.T, precision=lax.Precision.HIGHEST)

    stacked = lax.map(per_orbital, jnp.arange(NOCC, dtype=jnp.int32))
    return jnp.transpose(stacked, (1, 0, 2)).reshape(NAUXPAD, NOCC * NVIR)
```

```python
import jax
import jax.numpy as jnp
from jax import lax
from jax.sharding import Mesh, PartitionSpec as P

ZHI, Y, CORE, X, ZLO = 4, 4, 2, 4, 4
AXES = ("zh", "y", "c", "x", "zl")
FAST = lax.Precision.HIGH


def route(dz=0, dy=0, dc=0):
    pairs = []
    for zh in range(ZHI):
        for y in range(Y):
            for c in range(CORE):
                for x in range(X):
                    for zl in range(ZLO):
                        z = (zh * ZLO + zl + dz) % (ZHI * ZLO)
                        source = (((zh * Y + y) * CORE + c) * X + x) * ZLO + zl
                        target = (((z // ZLO * Y + (y + dy) % Y) * CORE + (c ^ dc)) * X + x) * ZLO + z % ZLO
                        pairs.append((source, target))
    return pairs


def moved(block, **delta):
    return lax.ppermute(block, AXES, route(**delta))


def gathered(block, axis):
    count = lax.axis_size(axis)
    return lax.all_to_all(jnp.broadcast_to(block[None], (count,) + block.shape), axis, 0, 0)


def in_order(own, ahead, across, behind, place):
    ring = jnp.stack([own, ahead, across, behind] * 2)
    return lax.dynamic_slice_in_dim(ring, (4 - place) % 4, 4, 0)


def both_cores(block, core):
    other = moved(block, dc=1)
    return jnp.where(core == 0, jnp.stack([block, other]), jnp.stack([other, block]))


def pick(blocks, place):
    return lax.dynamic_index_in_dim(blocks, place, 0, keepdims=False)


def shards(half_ints, virt_coeff, occ_energy, vir_energy, aux_sizes, pair_root):
    rows_dev, occ_grp, basis_count = half_ints.shape
    vir_count = virt_coeff.shape[1]
    zh, y, c, x, zl = (lax.axis_index(a) for a in AXES)
    width_dev = vir_count // ZLO

    coeff_rows = virt_coeff.shape[0] // CORE
    coeff = gathered(lax.dynamic_slice_in_dim(virt_coeff, c * coeff_rows, coeff_rows, 0), "x")
    coeff = in_order(coeff, moved(coeff, dz=-1), moved(coeff, dz=2), moved(coeff, dz=1), zl)
    coeff = both_cores(coeff, c)
    coeff = coeff.transpose(2, 1, 0, 3, 4).reshape(basis_count, vir_count)

    own_size = pick(aux_sizes, x * ZLO + zl)
    live_rows = (lax.iota(jnp.int32, rows_dev) < own_size).astype(jnp.float32)
    transformed = jnp.einsum("pim,ma->ipa", half_ints, coeff, precision=FAST, preferred_element_type=jnp.float32)
    transformed = transformed * live_rows[None, :, None]
    orbital_rows = lax.all_to_all(transformed, "x", 0, 0).reshape(X * rows_dev, vir_count)

    root = pick(pair_root, x)
    part_rows = X * rows_dev // (Y * CORE)
    parts = lax.all_to_all(orbital_rows.reshape(Y * CORE, part_rows, vir_count), ("y", "c"), 0, 0)
    part = pick(parts, root % (Y * CORE))
    slim = -(-part_rows // (8 * ZHI)) * 8
    thin = jnp.pad(part, ((0, slim * ZHI - part_rows), (0, 0))).reshape(ZHI, slim, vir_count)
    thin = pick(lax.all_to_all(thin, "zh", 0, 0), root // (Y * CORE))
    part = gathered(thin, "zh").reshape(ZHI * slim, vir_count)[:part_rows]
    partner = gathered(gathered(part, "zl"), "y")
    partner = both_cores(partner, c)
    partner = partner.transpose(1, 2, 0, 3, 4).reshape(X * ZLO * rows_dev, vir_count)

    held = orbital_rows.T.reshape(ZLO, width_dev, X * rows_dev)
    held = lax.all_to_all(held, "zl", 0, 0)
    held = held.reshape(ZLO, width_dev, X, rows_dev).transpose(1, 2, 0, 3).reshape(width_dev, X * ZLO * rows_dev)

    pair_rows = jnp.dot(held, partner, precision=FAST, preferred_element_type=jnp.float32)
    sent = pair_rows.reshape(width_dev, ZLO, width_dev).transpose(1, 0, 2)
    came = lax.all_to_all(sent, "zl", 0, 0)
    pair_cols = came.transpose(2, 0, 1).reshape(width_dev, vir_count)

    own_orbital = ((zh * Y + y) * CORE + c) * occ_grp + x
    partner_orbital = root * occ_grp + x
    occ_sum = pick(occ_energy, own_orbital) + pick(occ_energy, partner_orbital)
    vir_rows = lax.dynamic_slice_in_dim(vir_energy, zl * width_dev, width_dev)
    denominator = occ_sum - vir_rows[:, None] - vir_energy[None, :]
    amplitude = (2.0 * pair_rows - pair_cols) / denominator
    return jnp.dot(partner, amplitude.T, precision=FAST, preferred_element_type=jnp.float32)


def solution(mesh):
    fine = Mesh(mesh.devices.reshape(ZHI, Y, CORE, X, ZLO), AXES)
    groups, functions = ("zh", "y", "c"), ("x", "zl")
    return jax.shard_map(
        shards,
        mesh=fine,
        in_specs=(P(functions, groups, None), P(functions, None), P(), P(), P(), P()),
        out_specs=P(None, groups + functions),
        check_vma=False,
    )
```

```python
import jax
import jax.numpy as jnp
from jax import lax
from jax.sharding import Mesh, PartitionSpec as P

ZHI, Y, CORE, X, ZLO = 4, 4, 2, 4, 4
AXES = ("zh", "y", "c", "x", "zl")
FAST = lax.Precision.HIGH


def route(dz=0, dzh=0, dy=0, dc=0):
    pairs = []
    for zh in range(ZHI):
        for y in range(Y):
            for c in range(CORE):
                for x in range(X):
                    for zl in range(ZLO):
                        z = (zh * ZLO + zl + dz + dzh * ZLO) % (ZHI * ZLO)
                        source = (((zh * Y + y) * CORE + c) * X + x) * ZLO + zl
                        target = (((z // ZLO * Y + (y + dy) % Y) * CORE + (c ^ dc)) * X + x) * ZLO + z % ZLO
                        pairs.append((source, target))
    return pairs


def moved(block, **delta):
    return lax.ppermute(block, AXES, route(**delta))


def gathered(block, axis):
    count = lax.axis_size(axis)
    return lax.all_to_all(jnp.broadcast_to(block[None], (count,) + block.shape), axis, 0, 0)


def pick(blocks, place):
    return lax.dynamic_index_in_dim(blocks, place, 0, keepdims=False)


def ring_z(block):
    half = block.shape[-2] // 2
    ahead, behind = moved(block, dz=-1), moved(block, dz=1)
    low = moved(block[..., :half, :], dz=2)
    high = moved(block[..., half:, :], dz=-2)
    return [block, ahead, jnp.concatenate([low, high], -2), behind]


def ring_y(block):
    return [block, moved(block, dy=-1), moved(block, dy=2), moved(block, dy=1)]


def spread_zh(block, distance):
    half = block.shape[0] // 2
    up, down = moved(block, dzh=1), moved(block, dzh=-1)
    low, high = moved(up[:half], dzh=1), moved(down[half:], dzh=-1)
    across = jnp.concatenate([low, high], 0)
    return jnp.where(distance == 0, block, jnp.where(distance == 1, up, jnp.where(distance == 2, across, down)))


def rolled(ring, place):
    ring = jnp.stack(ring * 2)
    return lax.dynamic_slice_in_dim(ring, (4 - place) % 4, 4, 0)


def both_cores(block, other, core):
    return jnp.where(core == 0, jnp.stack([block, other]), jnp.stack([other, block]))


def feed_partner(half_ints, pair_root, y, c):
    rows_dev, slots, basis_count = half_ints.shape
    step = rows_dev // (Y * CORE * 4)
    split = half_ints.reshape(Y, step, CORE, 4, slots, basis_count)
    mine = lax.dynamic_index_in_dim(split, c, 2, keepdims=False)
    other = moved(lax.dynamic_index_in_dim(split, 1 - c, 2, keepdims=False), dc=1)
    root_core = (pair_root % CORE)[:, None]
    root_y = (pair_root // CORE % Y)[:, None]
    part = jnp.where(root_core == c, mine, other)
    parts = lax.all_to_all(part, "y", 0, 0)
    part = parts[0]
    for place in range(1, Y):
        part = jnp.where(root_y == place, parts[place], part)
    part = part.reshape(step * 4, slots, basis_count).transpose(1, 0, 2)
    return lax.all_to_all(part, "x", 0, 0).reshape(X * step * 4, basis_count)


def shards(half_ints, virt_coeff, occ_energy, vir_energy, aux_sizes, pair_root):
    rows_dev, occ_grp, basis_count = half_ints.shape
    vir_count = virt_coeff.shape[1]
    zh, y, c, x, zl = (lax.axis_index(a) for a in AXES)
    width_dev = vir_count // ZLO
    step = rows_dev // (Y * CORE * 4)
    root = pick(pair_root, x)

    coeff_rows = virt_coeff.shape[0] // CORE
    coeff = gathered(lax.dynamic_slice_in_dim(virt_coeff, c * coeff_rows, coeff_rows, 0), "x")
    raw = feed_partner(half_ints, pair_root, y, c)
    coeff = ring_z(coeff)
    coeff = rolled(coeff, zl)
    coeff = both_cores(coeff, moved(coeff, dc=1), c)
    coeff = coeff.transpose(2, 1, 0, 3, 4).reshape(basis_count, vir_count)

    part = jnp.dot(raw, coeff, precision=FAST, preferred_element_type=jnp.float32)
    sizes = lax.dynamic_index_in_dim(aux_sizes.reshape(X, ZLO), zl, 1)[:, :, None]
    place = y * (rows_dev // Y) + lax.iota(jnp.int32, step)[:, None] * 8 + c * 4 + lax.iota(jnp.int32, 4)[None, :]
    part = part * (place < sizes).astype(jnp.float32).reshape(-1, 1)
    part = spread_zh(part, (zh - root // (Y * CORE)) % ZHI)
    near = ring_y(rolled(ring_z(part), zl))
    far = [moved(r, dc=1) for r in near]
    partner = both_cores(rolled(near, y), rolled(far, y), c)
    partner = partner.reshape(CORE, Y, ZLO, X, step, 4, vir_count).transpose(3, 2, 1, 4, 0, 5, 6)
    partner = partner.reshape(X * ZLO * rows_dev, vir_count)

    own_size = pick(aux_sizes, x * ZLO + zl)
    live_rows = (lax.iota(jnp.int32, rows_dev) < own_size).astype(jnp.float32)
    transformed = jnp.einsum("pim,ma->ipa", half_ints, coeff, precision=FAST, preferred_element_type=jnp.float32)
    transformed = transformed * live_rows[None, :, None]
    orbital_rows = lax.all_to_all(transformed, "x", 0, 0).reshape(X * rows_dev, vir_count)
    held = orbital_rows.T.reshape(ZLO, width_dev, X * rows_dev)
    held = lax.all_to_all(held, "zl", 0, 0)
    held = held.reshape(ZLO, width_dev, X, rows_dev).transpose(1, 2, 0, 3).reshape(width_dev, X * ZLO * rows_dev)

    pair_rows = jnp.dot(held, partner, precision=FAST, preferred_element_type=jnp.float32)
    sent = pair_rows.reshape(width_dev, ZLO, width_dev).transpose(1, 0, 2)
    came = lax.all_to_all(sent, "zl", 0, 0)
    pair_cols = came.transpose(2, 0, 1).reshape(width_dev, vir_count)

    own_orbital = ((zh * Y + y) * CORE + c) * occ_grp + x
    partner_orbital = root * occ_grp + x
    occ_sum = pick(occ_energy, own_orbital) + pick(occ_energy, partner_orbital)
    vir_rows = lax.dynamic_slice_in_dim(vir_energy, zl * width_dev, width_dev)
    denominator = occ_sum - vir_rows[:, None] - vir_energy[None, :]
    amplitude = (2.0 * pair_rows - pair_cols) / denominator
    return jnp.dot(partner, amplitude.T, precision=FAST, preferred_element_type=jnp.float32)


def solution(mesh):
    fine = Mesh(mesh.devices.reshape(ZHI, Y, CORE, X, ZLO), AXES)
    groups, functions = ("zh", "y", "c"), ("x", "zl")
    return jax.shard_map(
        shards,
        mesh=fine,
        in_specs=(P(functions, groups, None), P(functions, None), P(), P(), P(), P()),
        out_specs=P(None, groups + functions),
        check_vma=False,
    )
```

```python
import jax
import jax.numpy as jnp
from jax import lax
from jax.experimental import pallas as pl
from jax.experimental.pallas import tpu as pltpu
from jax.sharding import Mesh, PartitionSpec as P


ZHI, Y, CORE, X, ZLO = 4, 4, 2, 4, 4
AXES = ("zh", "y", "c", "x", "zl")
FAST = lax.Precision.HIGH


def route(dz=0, dzh=0, dy=0, dc=0):
    pairs = []
    for zh in range(ZHI):
        for y in range(Y):
            for c in range(CORE):
                for x in range(X):
                    for zl in range(ZLO):
                        z = (zh * ZLO + zl + dz + dzh * ZLO) % (ZHI * ZLO)
                        source = (((zh * Y + y) * CORE + c) * X + x) * ZLO + zl
                        target = (((z // ZLO * Y + (y + dy) % Y) * CORE + (c ^ dc)) * X + x) * ZLO + z % ZLO
                        pairs.append((source, target))
    return pairs


def moved(block, **delta):
    return lax.ppermute(block, AXES, route(**delta))


def gathered(block, axis):
    count = lax.axis_size(axis)
    return lax.all_to_all(jnp.broadcast_to(block[None], (count,) + block.shape), axis, 0, 0)


def pick(blocks, place):
    return lax.dynamic_index_in_dim(blocks, place, 0, keepdims=False)


def ring_y(block):
    return [block, moved(block, dy=-1), moved(block, dy=2), moved(block, dy=1)]


def both_cores(block, other, core):
    return jnp.where(core == 0, jnp.stack([block, other]), jnp.stack([other, block]))


def own_core_part(half_ints, pair_root, c):
    rows_dev, slots, basis_count = half_ints.shape
    step = rows_dev // (Y * CORE * 4)
    split = half_ints.reshape(Y, step, CORE, 4, slots, basis_count)
    mine = lax.dynamic_index_in_dim(split, c, 2, keepdims=False)
    other = moved(lax.dynamic_index_in_dim(split, 1 - c, 2, keepdims=False), dc=1)
    return jnp.where((pair_root % CORE)[:, None] == c, mine, other)


def own_y_part(part, pair_root, y):
    distance = ((pair_root // CORE - y) % Y)[:, None]
    chosen = pick(part, y)
    for hop in range(1, Y):
        came = moved(pick(part, (y - hop) % Y), dy=-hop)
        chosen = jnp.where(distance == hop, came, chosen)
    return chosen.reshape(-1, *chosen.shape[2:]).transpose(1, 0, 2)


def split_float(value):
    high = value.astype(jnp.bfloat16)
    return high, (value - high.astype(jnp.float32)).astype(jnp.bfloat16)


def three_pass(left, right, dims):
    left_high, left_low = split_float(left)
    right_high, right_low = split_float(right)

    def product(p, q):
        return lax.dot_general(p, q, (dims, ((), ())), preferred_element_type=jnp.float32)

    return product(left_high, right_high) + product(left_high, right_low) + product(left_low, right_high)


def pair_kernel(place_ref, *refs):
    near, far, held_ref, pair_ref, partner_ref = refs[:Y], refs[Y : 2 * Y], refs[2 * Y], refs[2 * Y + 1], refs[2 * Y + 2]
    y, c = place_ref[0], place_ref[1]
    part_rows, vir_count = near[0].shape[1:]
    tiles = part_rows // 8
    band = 2 * part_rows // X
    lower = lax.broadcasted_iota(jnp.int32, (tiles, 8, vir_count), 1) < 4
    first = c == 0
    for hop in range(Y):
        mine = near[hop][0].reshape(tiles, 8, vir_count)
        other = far[hop][0].reshape(tiles, 8, vir_count)
        zero = jnp.where(first, mine, other)
        one = jnp.where(first, other, mine)
        even = jnp.where(lower, zero, pltpu.roll(one, 4, 1))
        odd = jnp.where(lower, pltpu.roll(zero, 4, 1), one)
        rows = jnp.stack([even, odd], 1).reshape(X, band, vir_count)
        start = pl.multiple_of(lax.rem(y + hop, Y) * band, 8)
        partner_ref[:, 0, pl.ds(start, band), :] = rows
    block = partner_ref[:, 0].reshape(X * Y * band, vir_count)
    product = three_pass(held_ref[0], block, ((1,), (0,)))

    @pl.when(pl.program_id(0) == 0)
    def _():
        pair_ref[...] = product

    @pl.when(pl.program_id(0) > 0)
    def _():
        pair_ref[...] += product


def pair_with_partner(near, far, held, y, c):
    part_rows, vir_count = near[0].shape[1:]
    width_dev, lanes = held.shape[1:]
    rows_dev = part_rows * Y * CORE // X
    part = pl.BlockSpec((1, part_rows, vir_count), lambda z: (z, 0, 0))
    pair, partner = pl.pallas_call(
        pair_kernel,
        grid=(ZLO,),
        out_shape=(
            jax.ShapeDtypeStruct((width_dev, vir_count), jnp.float32),
            jax.ShapeDtypeStruct((X, ZLO, rows_dev, vir_count), jnp.float32),
        ),
        in_specs=[pl.BlockSpec(memory_space=pltpu.SMEM)]
        + [part] * (2 * Y)
        + [pl.BlockSpec((1, width_dev, lanes), lambda z: (z, 0, 0))],
        out_specs=(
            pl.BlockSpec((width_dev, vir_count), lambda z: (0, 0)),
            pl.BlockSpec((X, 1, rows_dev, vir_count), lambda z: (0, z, 0, 0)),
        ),
        compiler_params=pltpu.CompilerParams(
            dimension_semantics=("arbitrary",), vmem_limit_bytes=24 << 20
        ),
        cost_estimate=pl.CostEstimate(
            flops=6 * width_dev * X * ZLO * rows_dev * vir_count, bytes_accessed=16 << 20, transcendentals=0
        ),
        name="pair_kernel",
    )(jnp.stack([y, c]).astype(jnp.int32), *(pltpu.with_memory_space_constraint(v, pltpu.HBM) for v in (*near, *far, held)))
    return pair, partner.reshape(X * ZLO * rows_dev, vir_count)


def shards(half_ints, virt_coeff, occ_energy, vir_energy, aux_sizes, pair_root):
    rows_dev, occ_grp, basis_count = half_ints.shape
    vir_count = virt_coeff.shape[1]
    zh, y, c, x, zl = (lax.axis_index(a) for a in AXES)
    width_dev = vir_count // ZLO
    step = rows_dev // (Y * CORE * 4)
    root = pick(pair_root, x)

    coeff_rows = virt_coeff.shape[0] // CORE
    coeff = gathered(lax.dynamic_slice_in_dim(virt_coeff, c * coeff_rows, coeff_rows, 0), "zl")
    raw = own_core_part(half_ints, pair_root, c)
    coeff, raw = lax.optimization_barrier((coeff, raw))
    raw = own_y_part(raw, pair_root, y)
    coeff = gathered(coeff, "x")
    raw = lax.all_to_all(raw, "x", 0, 0).reshape(X * step * 4, basis_count)
    coeff = both_cores(coeff, moved(coeff, dc=1), c)
    coeff = coeff.transpose(1, 2, 0, 3, 4).reshape(basis_count, vir_count)

    part = jnp.dot(raw, coeff, precision=FAST, preferred_element_type=jnp.float32)
    sizes = lax.dynamic_index_in_dim(aux_sizes.reshape(X, ZLO), zl, 1)[:, :, None]
    place = y * (rows_dev // Y) + lax.iota(jnp.int32, step)[:, None] * 8 + c * 4 + lax.iota(jnp.int32, 4)[None, :]
    part = part * (place < sizes).astype(jnp.float32).reshape(-1, 1)

    own_size = pick(aux_sizes, x * ZLO + zl)
    live_rows = (lax.iota(jnp.int32, rows_dev) < own_size).astype(jnp.float32)
    transformed = jnp.einsum("pim,ma->ipa", half_ints, coeff, precision=FAST, preferred_element_type=jnp.float32)
    transformed = transformed * live_rows[None, :, None]

    half = part.shape[0] // 2
    up, down = moved(part, dzh=1), moved(part, dzh=-1)
    up, down, transformed = lax.optimization_barrier((up, down, transformed))
    low, high = moved(up[:half], dzh=1), moved(down[half:], dzh=-1)
    orbital_rows = lax.all_to_all(transformed, "x", 0, 0).reshape(X * rows_dev, vir_count)
    distance = (zh - root // (Y * CORE)) % ZHI
    across = jnp.concatenate([low, high], 0)
    part = jnp.where(distance == 0, part, jnp.where(distance == 1, up, jnp.where(distance == 2, across, down)))
    near = gathered(part, "zl")
    near, orbital_rows = lax.optimization_barrier((near, orbital_rows))
    near = ring_y(near)
    far = [moved(r, dc=1) for r in near]

    held = orbital_rows.T.reshape(ZLO, width_dev, X * rows_dev)
    held = lax.all_to_all(held, "zl", 0, 0)

    pair_rows, partner = pair_with_partner(near, far, held, y, c)
    sent = pair_rows.reshape(width_dev, ZLO, width_dev).transpose(1, 0, 2)
    came = lax.all_to_all(sent, "zl", 0, 0)
    pair_cols = came.transpose(2, 0, 1).reshape(width_dev, vir_count)

    own_orbital = ((zh * Y + y) * CORE + c) * occ_grp + x
    partner_orbital = root * occ_grp + x
    occ_sum = pick(occ_energy, own_orbital) + pick(occ_energy, partner_orbital)
    vir_rows = lax.dynamic_slice_in_dim(vir_energy, zl * width_dev, width_dev)
    denominator = occ_sum - vir_rows[:, None] - vir_energy[None, :]
    amplitude = (2.0 * pair_rows - pair_cols) / denominator
    return jnp.dot(partner, amplitude.T, precision=FAST, preferred_element_type=jnp.float32)


def solution(mesh):
    fine = Mesh(mesh.devices.reshape(ZHI, Y, CORE, X, ZLO), AXES)
    groups, functions = ("zh", "y", "c"), ("x", "zl")
    return jax.shard_map(
        shards,
        mesh=fine,
        in_specs=(P(functions, groups, None), P(functions, None), P(), P(), P(), P()),
        out_specs=P(None, groups + functions),
        check_vma=False,
    )
```

```python
import jax
import jax.numpy as jnp
from jax import lax
from jax.experimental import pallas as pl
from jax.experimental.pallas import tpu as pltpu
from jax.sharding import Mesh, PartitionSpec as P


ZHI, Y, CORE, X, ZLO = 4, 4, 2, 4, 4
AXES = ("zh", "y", "c", "x", "zl")
FAST = lax.Precision.HIGH
LANES = 128


def route(dz=0, dzh=0, dy=0, dc=0):
    pairs = []
    for zh in range(ZHI):
        for y in range(Y):
            for c in range(CORE):
                for x in range(X):
                    for zl in range(ZLO):
                        z = (zh * ZLO + zl + dz + dzh * ZLO) % (ZHI * ZLO)
                        source = (((zh * Y + y) * CORE + c) * X + x) * ZLO + zl
                        target = (((z // ZLO * Y + (y + dy) % Y) * CORE + (c ^ dc)) * X + x) * ZLO + z % ZLO
                        pairs.append((source, target))
    return pairs


def moved(block, **delta):
    return lax.ppermute(block, AXES, route(**delta))


def gathered(block, axis):
    count = lax.axis_size(axis)
    return lax.all_to_all(jnp.broadcast_to(block[None], (count,) + block.shape), axis, 0, 0)


def pick(blocks, place):
    return lax.dynamic_index_in_dim(blocks, place, 0, keepdims=False)


def ring_y(block):
    return [block, moved(block, dy=-1), moved(block, dy=2), moved(block, dy=1)]


def both_cores(block, other, core):
    return jnp.where(core == 0, jnp.stack([block, other]), jnp.stack([other, block]))


def own_core_part(half_ints, pair_root, c):
    rows_dev, slots, basis_count = half_ints.shape
    step = rows_dev // (Y * CORE * 4)
    split = half_ints.reshape(Y, step, CORE, 4, slots, basis_count)
    mine = lax.dynamic_index_in_dim(split, c, 2, keepdims=False)
    other = moved(lax.dynamic_index_in_dim(split, 1 - c, 2, keepdims=False), dc=1)
    return jnp.where((pair_root % CORE)[:, None] == c, mine, other)


def own_y_part(part, pair_root, y):
    distance = ((pair_root // CORE - y) % Y)[:, None]
    chosen = pick(part, y)
    for hop in range(1, Y):
        came = moved(pick(part, (y - hop) % Y), dy=-hop)
        chosen = jnp.where(distance == hop, came, chosen)
    return chosen.reshape(-1, *chosen.shape[2:]).transpose(1, 0, 2)


def split_float(value):
    high = value.astype(jnp.bfloat16)
    return high, (value - high.astype(jnp.float32)).astype(jnp.bfloat16)


def three_pass(left, right, dims):
    def product(p, q):
        return lax.dot_general(p, q, (dims, ((), ())), preferred_element_type=jnp.float32)

    return product(left[0], right[0]) + product(left[0], right[1]) + product(left[1], right[0])


def pair_kernel(place_ref, *refs):
    near, far, held_ref = refs[:Y], refs[Y : 2 * Y], refs[2 * Y]
    pair_ref, sent_ref, high_ref, low_ref, rows_ref = refs[2 * Y + 1 :]
    y, c = place_ref[0], place_ref[1]
    part_rows, vir_count = near[0].shape[1:]
    tiles = part_rows // 8
    band = 2 * part_rows // X
    lower = lax.broadcasted_iota(jnp.int32, (tiles, 8, vir_count), 1) < 4
    first = c == 0
    for hop in range(Y):
        mine = near[hop][0].reshape(tiles, 8, vir_count)
        other = far[hop][0].reshape(tiles, 8, vir_count)
        zero = jnp.where(first, mine, other)
        one = jnp.where(first, other, mine)
        even = jnp.where(lower, zero, pltpu.roll(one, 4, 1))
        odd = jnp.where(lower, pltpu.roll(zero, 4, 1), one)
        rows = jnp.stack([even, odd], 1).reshape(X, band, vir_count)
        start = pl.multiple_of(lax.rem(y + hop, Y) * band, 8)
        rows_ref[:, pl.ds(start, band), :] = rows
    block = split_float(rows_ref[...].reshape(X * Y * band, vir_count))
    high_ref[:, 0] = block[0].reshape(X, Y * band, vir_count)
    low_ref[:, 0] = block[1].reshape(X, Y * band, vir_count)
    product = three_pass(split_float(held_ref[0]), block, ((1,), (0,)))
    step = pl.program_id(0)

    @pl.when(step == 0)
    def _():
        pair_ref[...] = product

    @pl.when(step > 0)
    def _():
        pair_ref[...] += product

    @pl.when(step == ZLO - 1)
    def _():
        width = pair_ref.shape[0]
        for target in range(ZLO):
            part = pair_ref[:, target * width : (target + 1) * width]
            sent_ref[target, :width] = part[:, :LANES]
            quarter = width // 4
            side = part[:, LANES:]
            sent_ref[target, width:] = jnp.concatenate(
                [side[g * quarter : (g + 1) * quarter] for g in range(4)], 1
            )


def pair_with_partner(near, far, held, y, c):
    part_rows, vir_count = near[0].shape[1:]
    width_dev, lanes = held.shape[1:]
    rows_dev = part_rows * Y * CORE // X
    packed = (ZLO, width_dev * width_dev // LANES, LANES)
    part = pl.BlockSpec((1, part_rows, vir_count), lambda z: (z, 0, 0))
    wide = pl.BlockSpec((X, 1, rows_dev, vir_count), lambda z: (0, z, 0, 0))
    operands = [pltpu.with_memory_space_constraint(v, pltpu.HBM) for v in (*near, *far, held)]
    return pl.pallas_call(
        pair_kernel,
        grid=(ZLO,),
        out_shape=(
            jax.ShapeDtypeStruct((width_dev, vir_count), jnp.float32),
            jax.ShapeDtypeStruct(packed, jnp.float32),
            pltpu.HBM((X, ZLO, rows_dev, vir_count), jnp.bfloat16),
            pltpu.HBM((X, ZLO, rows_dev, vir_count), jnp.bfloat16),
        ),
        in_specs=[pl.BlockSpec(memory_space=pltpu.SMEM)]
        + [part] * (2 * Y)
        + [pl.BlockSpec((1, width_dev, lanes), lambda z: (z, 0, 0))],
        out_specs=(
            pl.BlockSpec((width_dev, vir_count), lambda z: (0, 0)),
            pl.BlockSpec(packed, lambda z: (0, 0, 0)),
            wide,
            wide,
        ),
        scratch_shapes=[pltpu.VMEM((X, rows_dev, vir_count), jnp.float32)],
        compiler_params=pltpu.CompilerParams(dimension_semantics=("arbitrary",), vmem_limit_bytes=26 << 20),
        cost_estimate=pl.CostEstimate(
            flops=6 * width_dev * X * ZLO * rows_dev * vir_count, bytes_accessed=16 << 20, transcendentals=0
        ),
        name="pair_kernel",
    )(jnp.stack([y, c]).astype(jnp.int32), *operands)


def density_kernel(pair_ref, came_ref, row_ref, column_ref, high_ref, low_ref, gamma_ref, cols_ref, amp_ref):
    width = pair_ref.shape[0]

    @pl.when(pl.program_id(0) == 0)
    def _():
        quarter = width // 4
        fill = width - LANES
        cols_ref[...] = jnp.zeros_like(cols_ref)
        for source in range(ZLO):
            rows = slice(source * width, (source + 1) * width)
            cols_ref[rows, :LANES] = came_ref[source, :width]
            side = came_ref[source, width:]
            for g in range(4):
                part = slice(source * width + g * quarter, source * width + (g + 1) * quarter)
                cols_ref[part, LANES:width] = side[:, g * fill : (g + 1) * fill]
        columns = cols_ref[...].T[:width]
        amplitude = (2.0 * pair_ref[...] - columns) / (row_ref[...] - column_ref[...])
        high, low = split_float(amplitude)
        amp_ref[0] = high
        amp_ref[1] = low

    block = (high_ref[0].reshape(-1, high_ref.shape[-1]), low_ref[0].reshape(-1, low_ref.shape[-1]))
    gamma_ref[...] = three_pass((amp_ref[0], amp_ref[1]), block, ((1,), (1,)))


def densities(pair, came, row_part, column_part, high, low):
    width_dev, vir_count = pair.shape
    rows_dev = high.shape[2]
    whole = pl.BlockSpec((1, ZLO, rows_dev, vir_count), lambda x: (x, 0, 0, 0))
    return pl.pallas_call(
        density_kernel,
        grid=(X,),
        out_shape=jax.ShapeDtypeStruct((width_dev, X * ZLO * rows_dev), jnp.float32),
        in_specs=[
            pl.BlockSpec((width_dev, vir_count), lambda x: (0, 0)),
            pl.BlockSpec(came.shape, lambda x: (0, 0, 0)),
            pl.BlockSpec((width_dev, 1), lambda x: (0, 0)),
            pl.BlockSpec((1, vir_count), lambda x: (0, 0)),
            whole,
            whole,
        ],
        out_specs=pl.BlockSpec((width_dev, ZLO * rows_dev), lambda x: (0, x)),
        scratch_shapes=[
            pltpu.VMEM((ZLO * width_dev, 2 * LANES), jnp.float32),
            pltpu.VMEM((2, width_dev, vir_count), jnp.bfloat16),
        ],
        compiler_params=pltpu.CompilerParams(dimension_semantics=("arbitrary",), vmem_limit_bytes=20 << 20),
        cost_estimate=pl.CostEstimate(
            flops=6 * width_dev * X * ZLO * rows_dev * vir_count, bytes_accessed=10 << 20, transcendentals=0
        ),
        name="density_kernel",
    )(pair, came, row_part, column_part, *(pltpu.with_memory_space_constraint(v, pltpu.HBM) for v in (high, low)))


def shards(half_ints, virt_coeff, occ_energy, vir_energy, aux_sizes, pair_root):
    rows_dev, occ_grp, basis_count = half_ints.shape
    vir_count = virt_coeff.shape[1]
    zh, y, c, x, zl = (lax.axis_index(a) for a in AXES)
    width_dev = vir_count // ZLO
    step = rows_dev // (Y * CORE * 4)
    root = pick(pair_root, x)

    coeff_rows = virt_coeff.shape[0] // CORE
    coeff = gathered(lax.dynamic_slice_in_dim(virt_coeff, c * coeff_rows, coeff_rows, 0), "zl")
    raw = own_core_part(half_ints, pair_root, c)
    raw = own_y_part(raw, pair_root, y)
    coeff = gathered(coeff, "x")
    raw = lax.all_to_all(raw, "x", 0, 0).reshape(X * step * 4, basis_count)
    coeff = both_cores(coeff, moved(coeff, dc=1), c)
    coeff = coeff.transpose(1, 2, 0, 3, 4).reshape(basis_count, vir_count)

    part = jnp.dot(raw, coeff, precision=FAST, preferred_element_type=jnp.float32)
    sizes = lax.dynamic_index_in_dim(aux_sizes.reshape(X, ZLO), zl, 1)[:, :, None]
    place = y * (rows_dev // Y) + lax.iota(jnp.int32, step)[:, None] * 8 + c * 4 + lax.iota(jnp.int32, 4)[None, :]
    part = part * (place < sizes).astype(jnp.float32).reshape(-1, 1)

    own_size = pick(aux_sizes, x * ZLO + zl)
    live_rows = (lax.iota(jnp.int32, rows_dev) < own_size).astype(jnp.float32)
    transformed = jnp.einsum("pim,ma->ipa", half_ints, coeff, precision=FAST, preferred_element_type=jnp.float32)
    transformed = transformed * live_rows[None, :, None]

    half = part.shape[0] // 2
    up = moved(part, dzh=1)
    down = moved(part, dzh=-1)
    low, high = moved(up[:half], dzh=1), moved(down[half:], dzh=-1)
    orbital_rows = lax.all_to_all(transformed, "x", 0, 0).reshape(X * rows_dev, vir_count)
    distance = (zh - root // (Y * CORE)) % ZHI
    across = jnp.concatenate([low, high], 0)
    part = jnp.where(distance == 0, part, jnp.where(distance == 1, up, jnp.where(distance == 2, across, down)))
    near = gathered(part, "zl")
    near, orbital_rows = lax.optimization_barrier((near, orbital_rows))
    near = ring_y(near)
    far = [moved(r, dc=1) for r in near]

    held = orbital_rows.T.reshape(ZLO, width_dev, X * rows_dev)
    held = lax.all_to_all(held, "zl", 0, 0)

    pair_rows, sent, high, low = pair_with_partner(near, far, held, y, c)
    came = lax.all_to_all(sent, "zl", 0, 0)

    own_orbital = ((zh * Y + y) * CORE + c) * occ_grp + x
    partner_orbital = root * occ_grp + x
    occ_sum = pick(occ_energy, own_orbital) + pick(occ_energy, partner_orbital)
    vir_rows = lax.dynamic_slice_in_dim(vir_energy, zl * width_dev, width_dev)
    return densities(pair_rows, came, (occ_sum - vir_rows)[:, None], vir_energy[None, :], high, low).T


def solution(mesh):
    fine = Mesh(mesh.devices.reshape(ZHI, Y, CORE, X, ZLO), AXES)
    groups, functions = ("zh", "y", "c"), ("x", "zl")
    return jax.shard_map(
        shards,
        mesh=fine,
        in_specs=(P(functions, groups, None), P(functions, None), P(), P(), P(), P()),
        out_specs=P(None, groups + functions),
        check_vma=False,
    )
```

```python
import jax
import jax.numpy as jnp
from jax import lax
from jax.experimental import pallas as pl
from jax.experimental.pallas import tpu as pltpu
from jax.sharding import Mesh, PartitionSpec as P


ZHI, Y, CORE, X, ZLO = 4, 4, 2, 4, 4
AXES = ("zh", "y", "c", "x", "zl")
FAST = lax.Precision.HIGH
LANES = 128


def route(dz=0, dzh=0, dy=0, dc=0):
    pairs = []
    for zh in range(ZHI):
        for y in range(Y):
            for c in range(CORE):
                for x in range(X):
                    for zl in range(ZLO):
                        z = (zh * ZLO + zl + dz + dzh * ZLO) % (ZHI * ZLO)
                        source = (((zh * Y + y) * CORE + c) * X + x) * ZLO + zl
                        target = (((z // ZLO * Y + (y + dy) % Y) * CORE + (c ^ dc)) * X + x) * ZLO + z % ZLO
                        pairs.append((source, target))
    return pairs


def moved(block, **delta):
    return lax.ppermute(block, AXES, route(**delta))


def gathered(block, axis):
    count = lax.axis_size(axis)
    return lax.all_to_all(jnp.broadcast_to(block[None], (count,) + block.shape), axis, 0, 0)


def pick(blocks, place):
    return lax.dynamic_index_in_dim(blocks, place, 0, keepdims=False)


def ring_y(block):
    half = block.shape[0] // 2
    ahead, behind = moved(block, dy=-1), moved(block, dy=1)
    low = moved(behind[:half], dy=1)
    high = moved(ahead[half:], dy=-1)
    return [block, ahead, behind, low, high]


def both_cores(block, other, core):
    return jnp.where(core == 0, jnp.stack([block, other]), jnp.stack([other, block]))


def own_core_part(half_ints, pair_root, c):
    rows_dev, slots, basis_count = half_ints.shape
    step = rows_dev // (Y * CORE * 4)
    split = half_ints.reshape(Y, step, CORE, 4, slots, basis_count)
    mine = lax.dynamic_index_in_dim(split, c, 2, keepdims=False)
    other = moved(lax.dynamic_index_in_dim(split, 1 - c, 2, keepdims=False), dc=1)
    return jnp.where((pair_root % CORE)[:, None] == c, mine, other)


def own_part(part, root, here, axis):
    count = part.shape[0]
    distance = ((root - here) % count)[:, None]
    pieces = [pick(part, (here - hop) % count) for hop in range(count)]
    chosen = pieces[0]
    for hop in range(1, count):
        came = moved(pieces[hop], **{f"d{axis}": -hop})
        chosen = jnp.where(distance == hop, came, chosen)
    return chosen


def split_float(value):
    high = value.astype(jnp.bfloat16)
    return high, (value - high.astype(jnp.float32)).astype(jnp.bfloat16)


def three_pass(left, right, dims):
    def product(p, q):
        return lax.dot_general(p, q, (dims, ((), ())), preferred_element_type=jnp.float32)

    return product(left[0], right[0]) + product(left[0], right[1]) + product(left[1], right[0])


def pair_kernel(place_ref, *refs):
    near, far, held_ref = refs[:5], refs[5:10], refs[10]
    pair_ref, sent_ref, high_ref, low_ref, rows_ref = refs[11:]
    early = pl.program_id(0) < ZLO // 2
    y, c = place_ref[0], place_ref[1]
    part_rows, vir_count = near[0].shape[1:]
    tiles = part_rows // 8
    band = 2 * part_rows // X
    lower = lax.broadcasted_iota(jnp.int32, (tiles, 8, vir_count), 1) < 4
    first = c == 0

    def taken(parts, hop):
        if hop == 2:
            rows = jnp.where(early, parts[3][0], parts[4][0])
        else:
            rows = parts[(0, 1, 2, 2)[hop]][0]
        return rows.reshape(tiles, 8, vir_count)

    for hop in range(Y):
        mine = taken(near, hop)
        other = taken(far, hop)
        zero = jnp.where(first, mine, other)
        one = jnp.where(first, other, mine)
        even = jnp.where(lower, zero, pltpu.roll(one, 4, 1))
        odd = jnp.where(lower, pltpu.roll(zero, 4, 1), one)
        rows = jnp.stack([even, odd], 1).reshape(X, band, vir_count)
        start = pl.multiple_of(lax.rem(y + hop, Y) * band, 8)
        rows_ref[:, pl.ds(start, band), :] = rows
    block = split_float(rows_ref[...].reshape(X * Y * band, vir_count))
    high_ref[:, 0] = block[0].reshape(X, Y * band, vir_count)
    low_ref[:, 0] = block[1].reshape(X, Y * band, vir_count)
    product = three_pass(split_float(held_ref[0]), block, ((1,), (0,)))
    step = pl.program_id(0)

    @pl.when(step == 0)
    def _():
        pair_ref[...] = product

    @pl.when(step > 0)
    def _():
        pair_ref[...] += product

    @pl.when(step == ZLO - 1)
    def _():
        width = pair_ref.shape[0]
        for target in range(ZLO):
            part = pair_ref[:, target * width : (target + 1) * width]
            sent_ref[target, :width] = part[:, :LANES]
            quarter = width // 4
            side = part[:, LANES:]
            sent_ref[target, width:] = jnp.concatenate(
                [side[g * quarter : (g + 1) * quarter] for g in range(4)], 1
            )


def pair_with_partner(near, far, held, y, c):
    part_rows, vir_count = near[0].shape[1:]
    width_dev, lanes = held.shape[1:]
    rows_dev = part_rows * Y * CORE // X
    packed = (ZLO, width_dev * width_dev // LANES, LANES)
    part = pl.BlockSpec((1, part_rows, vir_count), lambda z: (z, 0, 0))
    wide = pl.BlockSpec((X, 1, rows_dev, vir_count), lambda z: (0, z, 0, 0))
    early = pl.BlockSpec((1, part_rows, vir_count), lambda z: (jnp.minimum(z, ZLO // 2 - 1), 0, 0))
    late = pl.BlockSpec((1, part_rows, vir_count), lambda z: (jnp.maximum(z - ZLO // 2, 0), 0, 0))
    operands = [pltpu.with_memory_space_constraint(v, pltpu.HBM) for v in (*near, *far)]
    return pl.pallas_call(
        pair_kernel,
        grid=(ZLO,),
        out_shape=(
            jax.ShapeDtypeStruct((width_dev, vir_count), jnp.float32),
            jax.ShapeDtypeStruct(packed, jnp.float32),
            pltpu.HBM((X, ZLO, rows_dev, vir_count), jnp.bfloat16),
            pltpu.HBM((X, ZLO, rows_dev, vir_count), jnp.bfloat16),
        ),
        in_specs=[pl.BlockSpec(memory_space=pltpu.SMEM)]
        + [part, part, part, early, late] * 2
        + [pl.BlockSpec((1, width_dev, lanes), lambda z: (z, 0, 0))],
        out_specs=(
            pl.BlockSpec((width_dev, vir_count), lambda z: (0, 0)),
            pl.BlockSpec(packed, lambda z: (0, 0, 0)),
            wide,
            wide,
        ),
        scratch_shapes=[pltpu.VMEM((X, rows_dev, vir_count), jnp.float32)],
        compiler_params=pltpu.CompilerParams(dimension_semantics=("arbitrary",), vmem_limit_bytes=26 << 20),
        cost_estimate=pl.CostEstimate(
            flops=6 * width_dev * X * ZLO * rows_dev * vir_count, bytes_accessed=16 << 20, transcendentals=0
        ),
        name="pair_kernel",
    )(jnp.stack([y, c]).astype(jnp.int32), *operands, held)


def density_kernel(pair_ref, came_ref, row_ref, column_ref, high_ref, low_ref, gamma_ref, cols_ref, amp_ref):
    width = pair_ref.shape[0]

    @pl.when(pl.program_id(0) == 0)
    def _():
        quarter = width // 4
        fill = width - LANES
        cols_ref[...] = jnp.zeros_like(cols_ref)
        for source in range(ZLO):
            rows = slice(source * width, (source + 1) * width)
            cols_ref[rows, :LANES] = came_ref[source, :width]
            side = came_ref[source, width:]
            for g in range(4):
                part = slice(source * width + g * quarter, source * width + (g + 1) * quarter)
                cols_ref[part, LANES:width] = side[:, g * fill : (g + 1) * fill]
        columns = cols_ref[...].T[:width]
        amplitude = (2.0 * pair_ref[...] - columns) / (row_ref[...] - column_ref[...])
        high, low = split_float(amplitude)
        amp_ref[0] = high
        amp_ref[1] = low

    block = (high_ref[0].reshape(-1, high_ref.shape[-1]), low_ref[0].reshape(-1, low_ref.shape[-1]))
    gamma_ref[...] = three_pass((amp_ref[0], amp_ref[1]), block, ((1,), (1,)))


def densities(pair, came, row_part, column_part, high, low):
    width_dev, vir_count = pair.shape
    rows_dev = high.shape[2]
    whole = pl.BlockSpec((1, ZLO, rows_dev, vir_count), lambda x: (x, 0, 0, 0))
    return pl.pallas_call(
        density_kernel,
        grid=(X,),
        out_shape=jax.ShapeDtypeStruct((width_dev, X * ZLO * rows_dev), jnp.float32),
        in_specs=[
            pl.BlockSpec((width_dev, vir_count), lambda x: (0, 0)),
            pl.BlockSpec(came.shape, lambda x: (0, 0, 0)),
            pl.BlockSpec((width_dev, 1), lambda x: (0, 0)),
            pl.BlockSpec((1, vir_count), lambda x: (0, 0)),
            whole,
            whole,
        ],
        out_specs=pl.BlockSpec((width_dev, ZLO * rows_dev), lambda x: (0, x)),
        scratch_shapes=[
            pltpu.VMEM((ZLO * width_dev, 2 * LANES), jnp.float32),
            pltpu.VMEM((2, width_dev, vir_count), jnp.bfloat16),
        ],
        compiler_params=pltpu.CompilerParams(dimension_semantics=("arbitrary",), vmem_limit_bytes=20 << 20),
        cost_estimate=pl.CostEstimate(
            flops=6 * width_dev * X * ZLO * rows_dev * vir_count, bytes_accessed=10 << 20, transcendentals=0
        ),
        name="density_kernel",
    )(pair, came, row_part, column_part, *(pltpu.with_memory_space_constraint(v, pltpu.HBM) for v in (high, low)))


def shards(half_ints, virt_coeff, occ_energy, vir_energy, aux_sizes, pair_root):
    rows_dev, occ_grp, basis_count = half_ints.shape
    vir_count = virt_coeff.shape[1]
    zh, y, c, x, zl = (lax.axis_index(a) for a in AXES)
    width_dev = vir_count // ZLO
    step = rows_dev // (Y * CORE * 4)
    root = pick(pair_root, x)

    coeff_rows = virt_coeff.shape[0] // CORE
    coeff = gathered(lax.dynamic_slice_in_dim(virt_coeff, c * coeff_rows, coeff_rows, 0), "zl")
    raw = own_core_part(half_ints, pair_root, c)
    raw = own_part(raw, pair_root // CORE % Y, y, "y")
    raw = raw.reshape(ZHI, step, occ_grp, basis_count)
    raw = own_part(raw, pair_root // (Y * CORE), zh, "zh").transpose(1, 0, 2)
    coeff = gathered(coeff, "x")
    raw = lax.all_to_all(raw, "x", 0, 0).reshape(X * step, basis_count)
    other = moved(coeff, dc=1)
    coeff = both_cores(coeff, other, c)
    coeff = coeff.transpose(1, 2, 0, 3, 4).reshape(basis_count, vir_count)

    part = jnp.dot(raw, coeff, precision=FAST, preferred_element_type=jnp.float32)
    sizes = lax.dynamic_index_in_dim(aux_sizes.reshape(X, ZLO), zl, 1)[:, :, None]
    row = zh * step + lax.iota(jnp.int32, step)[None, :, None]
    place = y * (rows_dev // Y) + row // 4 * 8 + c * 4 + row % 4
    part = part.reshape(X, step, vir_count) * (place < sizes).astype(jnp.float32)
    own_size = pick(aux_sizes, x * ZLO + zl)
    live_rows = (lax.iota(jnp.int32, rows_dev) < own_size).astype(jnp.float32)
    transformed = jnp.einsum("pim,ma->ipa", half_ints, coeff, precision=FAST, preferred_element_type=jnp.float32)
    transformed = transformed * live_rows[None, :, None]

    part = part.reshape(X * step, vir_count)
    ring = [part]
    for hop in range(1, ZHI):
        ring.append(moved(part, dzh=-hop))
    part = lax.dynamic_slice_in_dim(jnp.stack(ring * 2), (ZHI - zh) % ZHI, ZHI, 0)
    part = part.reshape(ZHI, X, step, vir_count).transpose(1, 0, 2, 3).reshape(X * ZHI * step, vir_count)
    orbital_rows = lax.all_to_all(transformed, "x", 0, 0).reshape(X * rows_dev, vir_count)
    near = gathered(part, "zl")
    near, orbital_rows = lax.optimization_barrier((near, orbital_rows))
    near = ring_y(near)
    far = [moved(r, dc=1) for r in near]

    held = orbital_rows.T.reshape(ZLO, width_dev, X * rows_dev)
    held = lax.all_to_all(held, "zl", 0, 0)

    pair_rows, sent, high, low = pair_with_partner(near, far, held, y, c)
    came = lax.all_to_all(sent, "zl", 0, 0)

    own_orbital = ((zh * Y + y) * CORE + c) * occ_grp + x
    partner_orbital = root * occ_grp + x
    occ_sum = pick(occ_energy, own_orbital) + pick(occ_energy, partner_orbital)
    vir_rows = lax.dynamic_slice_in_dim(vir_energy, zl * width_dev, width_dev)
    return densities(pair_rows, came, (occ_sum - vir_rows)[:, None], vir_energy[None, :], high, low).T


def solution(mesh):
    fine = Mesh(mesh.devices.reshape(ZHI, Y, CORE, X, ZLO), AXES)
    groups, functions = ("zh", "y", "c"), ("x", "zl")
    return jax.shard_map(
        shards,
        mesh=fine,
        in_specs=(P(functions, groups, None), P(functions, None), P(), P(), P(), P()),
        out_specs=P(None, groups + functions),
        check_vma=False,
    )
```

```python
import jax
import jax.numpy as jnp
from jax import lax
from jax.experimental import pallas as pl
from jax.experimental.layout import Layout, with_layout_constraint
from jax.experimental.pallas import tpu as pltpu
from jax.sharding import Mesh, PartitionSpec as P


ZHI, Y, CORE, X, ZLO = 4, 4, 2, 4, 4
AXES = ("zh", "y", "c", "x", "zl")
FAST = lax.Precision.HIGH
LANES = 128


def route(dz=0, dzh=0, dy=0, dc=0, dx=0):
    pairs = []
    for zh in range(ZHI):
        for y in range(Y):
            for c in range(CORE):
                for x in range(X):
                    for zl in range(ZLO):
                        z = (zh * ZLO + zl + dz + dzh * ZLO) % (ZHI * ZLO)
                        source = (((zh * Y + y) * CORE + c) * X + x) * ZLO + zl
                        target = (((z // ZLO * Y + (y + dy) % Y) * CORE + (c ^ dc)) * X + (x + dx) % X) * ZLO + z % ZLO
                        pairs.append((source, target))
    return pairs


def moved(block, **delta):
    return lax.ppermute(block, AXES, route(**delta))


def gathered(block, axis):
    count = lax.axis_size(axis)
    return lax.all_to_all(jnp.broadcast_to(block[None], (count,) + block.shape), axis, 0, 0)


def pick(blocks, place):
    return lax.dynamic_index_in_dim(blocks, place, 0, keepdims=False)


def ring_y(block):
    half = block.shape[0] // 2
    ahead, behind = moved(block, dy=-1), moved(block, dy=1)
    low = moved(behind[:half], dy=1)
    high = moved(ahead[half:], dy=-1)
    return [block, ahead, behind, low, high]


def own_core_part(half_ints, pair_root, c):
    rows_dev, slots, basis_count = half_ints.shape
    step = rows_dev // (Y * CORE * 4)
    split = half_ints.reshape(Y, step, CORE, 4, slots, basis_count)
    mine = lax.dynamic_index_in_dim(split, c, 2, keepdims=False)
    other = moved(lax.dynamic_index_in_dim(split, 1 - c, 2, keepdims=False), dc=1)
    return jnp.where((pair_root % CORE)[:, None] == c, mine, other)


def own_part(part, root, here, axis):
    count = part.shape[0]
    distance = ((root - here) % count)[:, None]
    pieces = [pick(part, (here - hop) % count) for hop in range(count)]
    chosen = pieces[0]
    for hop in range(1, count):
        came = moved(pieces[hop], **{f"d{axis}": -hop})
        chosen = jnp.where(distance == hop, came, chosen)
    return chosen


def split_float(value):
    high = value.astype(jnp.bfloat16)
    return high, (value - high.astype(jnp.float32)).astype(jnp.bfloat16)


def coefficient_kernel(place_ref, *refs):
    own, other, out_ref = refs[:X], refs[X : 2 * X], refs[2 * X]
    x, c = place_ref[0], place_ref[1]
    for hop in range(X):
        block = lax.rem(x + hop, X)
        out_ref[block, 0, c] = own[hop][0]
        out_ref[block, 0, 1 - c] = other[hop][0]


def coefficients(own, other, x, c):
    siblings, rows, vir_count = own[0].shape
    operands = [pltpu.with_memory_space_constraint(v, pltpu.HBM) for v in (*own, *other)]
    out = pl.pallas_call(
        coefficient_kernel,
        grid=(siblings,),
        out_shape=jax.ShapeDtypeStruct((X, siblings, CORE, rows, vir_count), jnp.float32),
        in_specs=[pl.BlockSpec(memory_space=pltpu.SMEM)]
        + [pl.BlockSpec((1, rows, vir_count), lambda z: (z, 0, 0))] * (2 * X),
        out_specs=pl.BlockSpec((X, 1, CORE, rows, vir_count), lambda z: (0, z, 0, 0, 0)),
        compiler_params=pltpu.CompilerParams(dimension_semantics=("arbitrary",), vmem_limit_bytes=8 << 20),
        cost_estimate=pl.CostEstimate(flops=0, bytes_accessed=8 << 20, transcendentals=0),
        name="coefficient_kernel",
    )(jnp.stack([x, c]).astype(jnp.int32), *operands)
    return out.reshape(X * siblings * CORE * rows, vir_count)


def three_pass(left, right, dims):
    def product(p, q):
        return lax.dot_general(p, q, (dims, ((), ())), preferred_element_type=jnp.float32)

    return product(left[0], right[0]) + product(left[0], right[1]) + product(left[1], right[0])


def pair_kernel(place_ref, *refs):
    near, far, held_ref = refs[:5], refs[5:10], refs[10]
    pair_ref, sent_ref, high_ref, low_ref, rows_ref = refs[11:]
    early = pl.program_id(0) < ZLO // 2
    y, c, x = place_ref[0], place_ref[1], place_ref[2]
    part_rows, vir_count = near[0].shape[1:]
    tiles = part_rows // 8
    band = 2 * part_rows // X
    lower = lax.broadcasted_iota(jnp.int32, (tiles, 8, vir_count), 1) < 4
    first = c == 0

    def taken(parts, hop):
        if hop == 2:
            rows = jnp.where(early, parts[3][0], parts[4][0])
        else:
            rows = parts[(0, 1, 2, 2)[hop]][0]
        return rows.reshape(tiles, 8, vir_count)

    for hop in range(Y):
        mine = taken(near, hop)
        other = taken(far, hop)
        zero = jnp.where(first, mine, other)
        one = jnp.where(first, other, mine)
        even = jnp.where(lower, zero, pltpu.roll(one, 4, 1))
        odd = jnp.where(lower, pltpu.roll(zero, 4, 1), one)
        rows = jnp.stack([even, odd], 1).reshape(X, band, vir_count)
        start = pl.multiple_of(lax.rem(y + hop, Y) * band, 8)
        rows_ref[:, pl.ds(start, band), :] = rows
    block = split_float(rows_ref[...].reshape(X * Y * band, vir_count))
    high_ref[:, 0] = block[0].reshape(X, Y * band, vir_count)
    low_ref[:, 0] = block[1].reshape(X, Y * band, vir_count)
    turned = [lax.rem(x + hop, X) for hop in range(X)]
    block = tuple(jnp.concatenate([ref[index, 0] for index in turned], 0) for ref in (high_ref, low_ref))
    product = three_pass(split_float(held_ref[0]), block, ((1,), (0,)))
    step = pl.program_id(0)

    @pl.when(step == 0)
    def _():
        pair_ref[...] = product

    @pl.when(step > 0)
    def _():
        pair_ref[...] += product

    @pl.when(step == ZLO - 1)
    def _():
        width = pair_ref.shape[0]
        for target in range(ZLO):
            part = pair_ref[:, target * width : (target + 1) * width]
            sent_ref[target, :width] = part[:, :LANES]
            quarter = width // 4
            side = part[:, LANES:]
            sent_ref[target, width:] = jnp.concatenate(
                [side[g * quarter : (g + 1) * quarter] for g in range(4)], 1
            )


def pair_with_partner(near, far, held, y, c, x):
    part_rows, vir_count = near[0].shape[1:]
    width_dev, lanes = held.shape[1:]
    rows_dev = part_rows * Y * CORE // X
    packed = (ZLO, width_dev * width_dev // LANES, LANES)
    part = pl.BlockSpec((1, part_rows, vir_count), lambda z: (z, 0, 0))
    wide = pl.BlockSpec((X, 1, rows_dev, vir_count), lambda z: (0, z, 0, 0))
    early = pl.BlockSpec((1, part_rows, vir_count), lambda z: (jnp.minimum(z, ZLO // 2 - 1), 0, 0))
    late = pl.BlockSpec((1, part_rows, vir_count), lambda z: (jnp.maximum(z - ZLO // 2, 0), 0, 0))
    operands = [pltpu.with_memory_space_constraint(v, pltpu.HBM) for v in (*near, *far)]
    return pl.pallas_call(
        pair_kernel,
        grid=(ZLO,),
        out_shape=(
            jax.ShapeDtypeStruct((width_dev, vir_count), jnp.float32),
            jax.ShapeDtypeStruct(packed, jnp.float32),
            pltpu.HBM((X, ZLO, rows_dev, vir_count), jnp.bfloat16),
            pltpu.HBM((X, ZLO, rows_dev, vir_count), jnp.bfloat16),
        ),
        in_specs=[pl.BlockSpec(memory_space=pltpu.SMEM)]
        + [part, part, part, early, late] * 2
        + [pl.BlockSpec((1, width_dev, lanes), lambda z: (z, 0, 0))],
        out_specs=(
            pl.BlockSpec((width_dev, vir_count), lambda z: (0, 0)),
            pl.BlockSpec(packed, lambda z: (0, 0, 0)),
            wide,
            wide,
        ),
        scratch_shapes=[pltpu.VMEM((X, rows_dev, vir_count), jnp.float32)],
        compiler_params=pltpu.CompilerParams(dimension_semantics=("arbitrary",), vmem_limit_bytes=26 << 20),
        cost_estimate=pl.CostEstimate(
            flops=6 * width_dev * X * ZLO * rows_dev * vir_count, bytes_accessed=16 << 20, transcendentals=0
        ),
        name="pair_kernel",
    )(jnp.stack([y, c, x]).astype(jnp.int32), *operands, held)


def density_kernel(pair_ref, came_ref, row_ref, column_ref, high_ref, low_ref, gamma_ref, cols_ref, amp_ref):
    width = pair_ref.shape[0]

    @pl.when(pl.program_id(0) == 0)
    def _():
        quarter = width // 4
        fill = width - LANES
        cols_ref[...] = jnp.zeros_like(cols_ref)
        for source in range(ZLO):
            rows = slice(source * width, (source + 1) * width)
            cols_ref[rows, :LANES] = came_ref[source, :width]
            side = came_ref[source, width:]
            for g in range(4):
                part = slice(source * width + g * quarter, source * width + (g + 1) * quarter)
                cols_ref[part, LANES:width] = side[:, g * fill : (g + 1) * fill]
        columns = cols_ref[...].T[:width]
        amplitude = (2.0 * pair_ref[...] - columns) / (row_ref[...] - column_ref[...])
        high, low = split_float(amplitude)
        amp_ref[0] = high
        amp_ref[1] = low

    block = (high_ref[0].reshape(-1, high_ref.shape[-1]), low_ref[0].reshape(-1, low_ref.shape[-1]))
    gamma_ref[...] = three_pass((amp_ref[0], amp_ref[1]), block, ((1,), (1,)))


def densities(pair, came, row_part, column_part, high, low):
    width_dev, vir_count = pair.shape
    rows_dev = high.shape[2]
    whole = pl.BlockSpec((1, ZLO, rows_dev, vir_count), lambda x: (x, 0, 0, 0))
    return pl.pallas_call(
        density_kernel,
        grid=(X,),
        out_shape=jax.ShapeDtypeStruct((width_dev, X * ZLO * rows_dev), jnp.float32),
        in_specs=[
            pl.BlockSpec((width_dev, vir_count), lambda x: (0, 0)),
            pl.BlockSpec(came.shape, lambda x: (0, 0, 0)),
            pl.BlockSpec((width_dev, 1), lambda x: (0, 0)),
            pl.BlockSpec((1, vir_count), lambda x: (0, 0)),
            whole,
            whole,
        ],
        out_specs=pl.BlockSpec((width_dev, ZLO * rows_dev), lambda x: (0, x)),
        scratch_shapes=[
            pltpu.VMEM((ZLO * width_dev, 2 * LANES), jnp.float32),
            pltpu.VMEM((2, width_dev, vir_count), jnp.bfloat16),
        ],
        compiler_params=pltpu.CompilerParams(dimension_semantics=("arbitrary",), vmem_limit_bytes=20 << 20),
        cost_estimate=pl.CostEstimate(
            flops=6 * width_dev * X * ZLO * rows_dev * vir_count, bytes_accessed=10 << 20, transcendentals=0
        ),
        name="density_kernel",
    )(pair, came, row_part, column_part, *(pltpu.with_memory_space_constraint(v, pltpu.HBM) for v in (high, low)))


def shards(half_ints, virt_coeff, occ_energy, vir_energy, aux_sizes, pair_root):
    rows_dev, occ_grp, basis_count = half_ints.shape
    vir_count = virt_coeff.shape[1]
    zh, y, c, x, zl = (lax.axis_index(a) for a in AXES)
    width_dev = vir_count // ZLO
    step = rows_dev // (Y * CORE * 4)
    root = pick(pair_root, x)

    coeff_rows = virt_coeff.shape[0] // CORE
    coeff = gathered(lax.dynamic_slice_in_dim(virt_coeff, c * coeff_rows, coeff_rows, 0), "zl")
    raw = own_core_part(half_ints, pair_root, c)
    raw = own_part(raw, pair_root // CORE % Y, y, "y")
    raw = raw.reshape(ZHI, step, occ_grp, basis_count)
    root_zh = (pair_root // (Y * CORE))[:, None]
    parts = lax.all_to_all(raw, "zh", 0, 0)
    raw = parts[0]
    for place in range(1, ZHI):
        raw = jnp.where(root_zh == place, parts[place], raw)
    raw = raw.transpose(1, 0, 2)
    ring = [coeff]
    for hop in range(1, X):
        ring.append(moved(coeff, dx=-hop))
    raw = lax.all_to_all(raw, "x", 0, 0).reshape(X * step, basis_count)
    other = []
    for block in ring:
        other.append(moved(block, dc=1))
    coeff = coefficients(ring, other, x, c)

    part = jnp.dot(raw, coeff, precision=FAST, preferred_element_type=jnp.float32)
    sizes = lax.dynamic_index_in_dim(aux_sizes.reshape(X, ZLO), zl, 1)[:, :, None]
    row = zh * step + lax.iota(jnp.int32, step)[None, :, None]
    place = y * (rows_dev // Y) + row // 4 * 8 + c * 4 + row % 4
    part = part.reshape(X, step, vir_count) * (place < sizes).astype(jnp.float32)
    own_size = pick(aux_sizes, x * ZLO + zl)
    live_rows = (lax.iota(jnp.int32, rows_dev) < own_size).astype(jnp.float32)
    transformed = jnp.einsum("pim,ma->ipa", half_ints, coeff, precision=FAST, preferred_element_type=jnp.float32)
    transformed = with_layout_constraint(transformed * live_rows[None, :, None], Layout((0, 1, 2)))

    part = part.reshape(X * step, vir_count)
    part = gathered(part, "zh")
    part = part.reshape(ZHI, X, step, vir_count).transpose(1, 0, 2, 3).reshape(X * ZHI * step, vir_count)
    owned = [pick(transformed, x)]
    for hop in range(1, X):
        owned.append(moved(pick(transformed, (x - hop) % X), dx=-hop))
    orbital_rows = jnp.concatenate(owned, 0)
    near = gathered(part, "zl")
    held = orbital_rows.T.reshape(ZLO, width_dev, X * rows_dev)
    near, held = lax.optimization_barrier((near, held))
    near = ring_y(near)
    far = [moved(r, dc=1) for r in near]
    held = lax.all_to_all(held, "zl", 0, 0)

    pair_rows, sent, high, low = pair_with_partner(near, far, held, y, c, x)
    came = lax.all_to_all(sent, "zl", 0, 0)

    own_orbital = ((zh * Y + y) * CORE + c) * occ_grp + x
    partner_orbital = root * occ_grp + x
    occ_sum = pick(occ_energy, own_orbital) + pick(occ_energy, partner_orbital)
    vir_rows = lax.dynamic_slice_in_dim(vir_energy, zl * width_dev, width_dev)
    return densities(pair_rows, came, (occ_sum - vir_rows)[:, None], vir_energy[None, :], high, low).T


def solution(mesh):
    fine = Mesh(mesh.devices.reshape(ZHI, Y, CORE, X, ZLO), AXES)
    groups, functions = ("zh", "y", "c"), ("x", "zl")
    return jax.shard_map(
        shards,
        mesh=fine,
        in_specs=(P(functions, groups, None), P(functions, None), P(), P(), P(), P()),
        out_specs=P(None, groups + functions),
        check_vma=False,
    )
```

```python
import jax
import jax.numpy as jnp
from jax import lax
from jax.experimental import pallas as pl
from jax.experimental.layout import Layout, with_layout_constraint
from jax.experimental.pallas import tpu as pltpu
from jax.sharding import Mesh, PartitionSpec as P


ZHI, Y, CORE, X, ZLO = 4, 4, 2, 4, 4
AXES = ("zh", "y", "c", "x", "zl")
FAST = lax.Precision.HIGH
LANES = 128


def route(dz=0, dzh=0, dy=0, dc=0, dx=0):
    pairs = []
    for zh in range(ZHI):
        for y in range(Y):
            for c in range(CORE):
                for x in range(X):
                    for zl in range(ZLO):
                        z = (zh * ZLO + zl + dz + dzh * ZLO) % (ZHI * ZLO)
                        source = (((zh * Y + y) * CORE + c) * X + x) * ZLO + zl
                        target = (((z // ZLO * Y + (y + dy) % Y) * CORE + (c ^ dc)) * X + (x + dx) % X) * ZLO + z % ZLO
                        pairs.append((source, target))
    return pairs


def moved(block, **delta):
    return lax.ppermute(block, AXES, route(**delta))


def gathered(block, axis):
    count = lax.axis_size(axis)
    return lax.all_to_all(jnp.broadcast_to(block[None], (count,) + block.shape), axis, 0, 0)


def pick(blocks, place):
    return lax.dynamic_index_in_dim(blocks, place, 0, keepdims=False)


def ring_y(block):
    half = block.shape[0] // 2
    ahead = moved(block, dy=-1)
    behind = moved(block, dy=1)
    low = moved(behind[:half], dy=1)
    high = moved(ahead[half:], dy=-1)
    return [block, ahead, behind, low, high]


def own_core_part(half_ints, pair_root, c):
    rows_dev, slots, basis_count = half_ints.shape
    step = rows_dev // (Y * CORE * 4)
    split = half_ints.reshape(Y, step, CORE, 4, slots, basis_count)
    mine = lax.dynamic_index_in_dim(split, c, 2, keepdims=False)
    other = moved(lax.dynamic_index_in_dim(split, 1 - c, 2, keepdims=False), dc=1)
    return jnp.where((pair_root % CORE)[:, None] == c, mine, other)


def own_part(part, root, here, axis):
    count = part.shape[0]
    distance = ((root - here) % count)[:, None]
    pieces = [pick(part, (here - hop) % count) for hop in range(count)]
    chosen = pieces[0]
    for hop in range(1, count):
        came = moved(pieces[hop], **{f"d{axis}": -hop})
        chosen = jnp.where(distance == hop, came, chosen)
    return chosen


def split_float(value):
    high = value.astype(jnp.bfloat16)
    return high, (value - high.astype(jnp.float32)).astype(jnp.bfloat16)


def coefficient_kernel(place_ref, *refs):
    own, other, out_ref = refs[:X], refs[X : 2 * X], refs[2 * X]
    x, c = place_ref[0], place_ref[1]
    for hop in range(X):
        block = lax.rem(x + hop, X)
        out_ref[block, 0, c] = own[hop][0]
        out_ref[block, 0, 1 - c] = other[hop][0]


def coefficients(own, other, x, c):
    siblings, rows, vir_count = own[0].shape
    operands = [pltpu.with_memory_space_constraint(v, pltpu.HBM) for v in (*own, *other)]
    out = pl.pallas_call(
        coefficient_kernel,
        grid=(siblings,),
        out_shape=jax.ShapeDtypeStruct((X, siblings, CORE, rows, vir_count), jnp.float32),
        in_specs=[pl.BlockSpec(memory_space=pltpu.SMEM)]
        + [pl.BlockSpec((1, rows, vir_count), lambda z: (z, 0, 0))] * (2 * X),
        out_specs=pl.BlockSpec((X, 1, CORE, rows, vir_count), lambda z: (0, z, 0, 0, 0)),
        compiler_params=pltpu.CompilerParams(dimension_semantics=("arbitrary",), vmem_limit_bytes=8 << 20),
        cost_estimate=pl.CostEstimate(flops=0, bytes_accessed=8 << 20, transcendentals=0),
        name="coefficient_kernel",
    )(jnp.stack([x, c]).astype(jnp.int32), *operands)
    return out.reshape(X * siblings * CORE * rows, vir_count)


def three_pass(left, right, dims):
    def product(p, q):
        return lax.dot_general(p, q, (dims, ((), ())), preferred_element_type=jnp.float32)

    return product(left[0], right[0]) + product(left[0], right[1]) + product(left[1], right[0])


def pair_kernel(place_ref, *refs):
    near, far, held_ref = refs[:5], refs[5:10], refs[10]
    pair_ref, sent_ref, high_ref, low_ref, rows_ref = refs[11:]
    early = pl.program_id(0) < ZLO // 2
    y, c, x = place_ref[0], place_ref[1], place_ref[2]
    part_rows, vir_count = near[0].shape[1:]
    tiles = part_rows // 8
    band = 2 * part_rows // X
    lower = lax.broadcasted_iota(jnp.int32, (tiles, 8, vir_count), 1) < 4
    first = c == 0

    def taken(parts, hop):
        if hop == 2:
            rows = jnp.where(early, parts[3][0], parts[4][0])
        else:
            rows = parts[(0, 1, 2, 2)[hop]][0]
        return rows.reshape(tiles, 8, vir_count)

    for hop in range(Y):
        mine = taken(near, hop)
        other = taken(far, hop)
        zero = jnp.where(first, mine, other)
        one = jnp.where(first, other, mine)
        even = jnp.where(lower, zero, pltpu.roll(one, 4, 1))
        odd = jnp.where(lower, pltpu.roll(zero, 4, 1), one)
        rows = jnp.stack([even, odd], 1).reshape(X, band, vir_count)
        start = pl.multiple_of(lax.rem(y + hop, Y) * band, 8)
        rows_ref[:, pl.ds(start, band), :] = rows
    block = split_float(rows_ref[...].reshape(X * Y * band, vir_count))
    high_ref[:, 0] = block[0].reshape(X, Y * band, vir_count)
    low_ref[:, 0] = block[1].reshape(X, Y * band, vir_count)
    turned = [lax.rem(x + hop, X) for hop in range(X)]
    block = tuple(jnp.concatenate([ref[index, 0] for index in turned], 0) for ref in (high_ref, low_ref))
    product = three_pass(split_float(held_ref[0]), block, ((1,), (0,)))
    step = pl.program_id(0)

    @pl.when(step == 0)
    def _():
        pair_ref[...] = product

    @pl.when(step > 0)
    def _():
        pair_ref[...] += product

    @pl.when(step == ZLO - 1)
    def _():
        width = pair_ref.shape[0]
        for target in range(ZLO):
            part = pair_ref[:, target * width : (target + 1) * width]
            sent_ref[target, :width] = part[:, :LANES]
            quarter = width // 4
            side = part[:, LANES:]
            sent_ref[target, width:] = jnp.concatenate(
                [side[g * quarter : (g + 1) * quarter] for g in range(4)], 1
            )


def pair_with_partner(near, far, held, y, c, x):
    part_rows, vir_count = near[0].shape[1:]
    width_dev, lanes = held.shape[1:]
    rows_dev = part_rows * Y * CORE // X
    packed = (ZLO, width_dev * width_dev // LANES, LANES)
    part = pl.BlockSpec((1, part_rows, vir_count), lambda z: (z, 0, 0))
    wide = pl.BlockSpec((X, 1, rows_dev, vir_count), lambda z: (0, z, 0, 0))
    early = pl.BlockSpec((1, part_rows, vir_count), lambda z: (jnp.minimum(z, ZLO // 2 - 1), 0, 0))
    late = pl.BlockSpec((1, part_rows, vir_count), lambda z: (jnp.maximum(z - ZLO // 2, 0), 0, 0))
    operands = [pltpu.with_memory_space_constraint(v, pltpu.HBM) for v in (*near, *far)]
    return pl.pallas_call(
        pair_kernel,
        grid=(ZLO,),
        out_shape=(
            jax.ShapeDtypeStruct((width_dev, vir_count), jnp.float32),
            jax.ShapeDtypeStruct(packed, jnp.float32),
            pltpu.HBM((X, ZLO, rows_dev, vir_count), jnp.bfloat16),
            pltpu.HBM((X, ZLO, rows_dev, vir_count), jnp.bfloat16),
        ),
        in_specs=[pl.BlockSpec(memory_space=pltpu.SMEM)]
        + [part, part, part, early, late] * 2
        + [pl.BlockSpec((1, width_dev, lanes), lambda z: (z, 0, 0))],
        out_specs=(
            pl.BlockSpec((width_dev, vir_count), lambda z: (0, 0)),
            pl.BlockSpec(packed, lambda z: (0, 0, 0)),
            wide,
            wide,
        ),
        scratch_shapes=[pltpu.VMEM((X, rows_dev, vir_count), jnp.float32)],
        compiler_params=pltpu.CompilerParams(dimension_semantics=("arbitrary",), vmem_limit_bytes=26 << 20),
        cost_estimate=pl.CostEstimate(
            flops=6 * width_dev * X * ZLO * rows_dev * vir_count, bytes_accessed=16 << 20, transcendentals=0
        ),
        name="pair_kernel",
    )(jnp.stack([y, c, x]).astype(jnp.int32), *operands, held)


def density_kernel(pair_ref, came_ref, row_ref, column_ref, high_ref, low_ref, gamma_ref, cols_ref, amp_ref):
    width = pair_ref.shape[0]

    @pl.when(pl.program_id(0) == 0)
    def _():
        quarter = width // 4
        fill = width - LANES
        cols_ref[...] = jnp.zeros_like(cols_ref)
        for source in range(ZLO):
            rows = slice(source * width, (source + 1) * width)
            cols_ref[rows, :LANES] = came_ref[source, :width]
            side = came_ref[source, width:]
            for g in range(4):
                part = slice(source * width + g * quarter, source * width + (g + 1) * quarter)
                cols_ref[part, LANES:width] = side[:, g * fill : (g + 1) * fill]
        columns = cols_ref[...].T[:width]
        amplitude = (2.0 * pair_ref[...] - columns) / (row_ref[...] - column_ref[...])
        high, low = split_float(amplitude)
        amp_ref[0] = high
        amp_ref[1] = low

    block = (high_ref[0].reshape(-1, high_ref.shape[-1]), low_ref[0].reshape(-1, low_ref.shape[-1]))
    gamma_ref[...] = three_pass((amp_ref[0], amp_ref[1]), block, ((1,), (1,)))


def densities(pair, came, row_part, column_part, high, low):
    width_dev, vir_count = pair.shape
    rows_dev = high.shape[2]
    whole = pl.BlockSpec((1, ZLO, rows_dev, vir_count), lambda x: (x, 0, 0, 0))
    return pl.pallas_call(
        density_kernel,
        grid=(X,),
        out_shape=jax.ShapeDtypeStruct((width_dev, X * ZLO * rows_dev), jnp.float32),
        in_specs=[
            pl.BlockSpec((width_dev, vir_count), lambda x: (0, 0)),
            pl.BlockSpec(came.shape, lambda x: (0, 0, 0)),
            pl.BlockSpec((width_dev, 1), lambda x: (0, 0)),
            pl.BlockSpec((1, vir_count), lambda x: (0, 0)),
            whole,
            whole,
        ],
        out_specs=pl.BlockSpec((width_dev, ZLO * rows_dev), lambda x: (0, x)),
        scratch_shapes=[
            pltpu.VMEM((ZLO * width_dev, 2 * LANES), jnp.float32),
            pltpu.VMEM((2, width_dev, vir_count), jnp.bfloat16),
        ],
        compiler_params=pltpu.CompilerParams(dimension_semantics=("arbitrary",), vmem_limit_bytes=20 << 20),
        cost_estimate=pl.CostEstimate(
            flops=6 * width_dev * X * ZLO * rows_dev * vir_count, bytes_accessed=10 << 20, transcendentals=0
        ),
        name="density_kernel",
    )(pair, came, row_part, column_part, *(pltpu.with_memory_space_constraint(v, pltpu.HBM) for v in (high, low)))


def shards(half_ints, virt_coeff, occ_energy, vir_energy, aux_sizes, pair_root):
    rows_dev, occ_grp, basis_count = half_ints.shape
    vir_count = virt_coeff.shape[1]
    zh, y, c, x, zl = (lax.axis_index(a) for a in AXES)
    width_dev = vir_count // ZLO
    step = rows_dev // (Y * CORE * 4)
    root = pick(pair_root, x)

    coeff_rows = virt_coeff.shape[0] // CORE
    coeff = gathered(lax.dynamic_slice_in_dim(virt_coeff, c * coeff_rows, coeff_rows, 0), "zl")
    raw = own_core_part(half_ints, pair_root, c)
    raw = own_part(raw, pair_root // CORE % Y, y, "y")
    raw = raw.reshape(ZHI, step, occ_grp, basis_count)
    root_zh = (pair_root // (Y * CORE))[:, None]
    parts = lax.all_to_all(raw, "zh", 0, 0)
    raw = parts[0]
    for place in range(1, ZHI):
        raw = jnp.where(root_zh == place, parts[place], raw)
    raw = raw.transpose(1, 0, 2)
    ring = [coeff]
    for hop in range(1, X):
        ring.append(moved(coeff, dx=-hop))
    raw = lax.all_to_all(raw, "x", 0, 0).reshape(X * step, basis_count)
    other = []
    for block in ring:
        other.append(moved(block, dc=1))
    coeff = coefficients(ring, other, x, c)

    part = jnp.dot(raw, coeff, precision=FAST, preferred_element_type=jnp.float32)
    sizes = lax.dynamic_index_in_dim(aux_sizes.reshape(X, ZLO), zl, 1)[:, :, None]
    row = zh * step + lax.iota(jnp.int32, step)[None, :, None]
    place = y * (rows_dev // Y) + row // 4 * 8 + c * 4 + row % 4
    part = part.reshape(X, step, vir_count) * (place < sizes).astype(jnp.float32)
    own_size = pick(aux_sizes, x * ZLO + zl)
    live_rows = (lax.iota(jnp.int32, rows_dev) < own_size).astype(jnp.float32)
    transformed = jnp.einsum("pim,ma->ipa", half_ints, coeff, precision=FAST, preferred_element_type=jnp.float32)
    transformed = with_layout_constraint(transformed * live_rows[None, :, None], Layout((0, 1, 2)))

    part = part.reshape(step, X, vir_count)
    near = lax.all_to_all(jnp.broadcast_to(part[None], (ZHI * ZLO,) + part.shape), ("zh", "zl"), 0, 0)
    near = near.reshape(ZHI, ZLO, X, step, vir_count).transpose(1, 2, 0, 3, 4).reshape(ZLO, X * ZHI * step, vir_count)
    owned = [pick(transformed, x)]
    for hop in range(1, X):
        owned.append(moved(pick(transformed, (x - hop) % X), dx=-hop))
    orbital_rows = jnp.concatenate(owned, 0)
    held = orbital_rows.T.reshape(ZLO, width_dev, X * rows_dev)
    near, held = lax.optimization_barrier((near, held))
    near = ring_y(near)
    far = [moved(r, dc=1) for r in near]
    held = lax.all_to_all(held, "zl", 0, 0)

    pair_rows, sent, high, low = pair_with_partner(near, far, held, y, c, x)
    came = lax.all_to_all(sent, "zl", 0, 0)

    own_orbital = ((zh * Y + y) * CORE + c) * occ_grp + x
    partner_orbital = root * occ_grp + x
    occ_sum = pick(occ_energy, own_orbital) + pick(occ_energy, partner_orbital)
    vir_rows = lax.dynamic_slice_in_dim(vir_energy, zl * width_dev, width_dev)
    return densities(pair_rows, came, (occ_sum - vir_rows)[:, None], vir_energy[None, :], high, low).T


def solution(mesh):
    fine = Mesh(mesh.devices.reshape(ZHI, Y, CORE, X, ZLO), AXES)
    groups, functions = ("zh", "y", "c"), ("x", "zl")
    return jax.shard_map(
        shards,
        mesh=fine,
        in_specs=(P(functions, groups, None), P(functions, None), P(), P(), P(), P()),
        out_specs=P(None, groups + functions),
        check_vma=False,
    )
```
